32 devices in a mesh: ep: 8 (over z, y), dp: 4 (over x, core).
Axes of the slice: x: 2, y: 2, z: 4, core: 2. Of those that a mesh axis runs over, the one named last changes fastest.
Arguments:
- out_grads: bfloat16 [4096, 2048], P(('ep', 'dp')), may hold values from -40 to 40
- hidden_acts: bfloat16 [4096, 512], P(('ep', 'dp')), may hold values from -20 to 20
- routing: int32 [4096, 1], P(('ep', 'dp')), may hold values from 0 to 5, as said below
- replica_pick: int32 [4096], P(('ep', 'dp')), may hold values from 0 to 3
- master_weights: float32 [8, 2048, 512], P('ep', 'dp'), may hold values from -0.25 to 0.25
- current_slots: int32 [8], replicated, may hold values from 0 to 5, as said below
- next_slots: int32 [8], replicated, may hold values from 0 to 5, as said below
Outputs:
- input_grads: float32 [4096, 512], P(('ep', 'dp'))
- moved_weights: float32 [8, 2048, 512], P('ep', 'dp')
- moved_updates: float32 [8, 2048, 512], P('ep', 'dp')
The draws below stay inside these ranges and needn't reach their ends.
Inputs may be any that keep to these rules, and one draw needn't show every extreme that they name: `routing`: the rows of one device name each expert at most 32 times; the experts held by two slots now are named exactly 32 times by the rows of every device. `current_slots`: every expert below 6 is held by one or two slots. `next_slots`: every expert below 6 is held by at least one slot.
All inputs are finite; a program needn't handle non-finite values.
Results may differ from the reference program's by a relative error of at most 0.0029.
Values may be sent and summed in bfloat16 or wider, within the bound.
No kernel may reach another device: no remote copies, remote signals or barrier semaphores. Data moves between devices by JAX's collectives and lax.ppermute only.
A program may use at most 64 MiB of HBM per device.

```python
import jax
import jax.numpy as jnp
from jax import lax

D = 2048
F = 512
TOK_DEV = 128
NS_STEPS = 2
EXPERTS = 6
CAP = 32
TOKENS = 4096
N_EP = 8
N_DP = 4


def draw_out_grads(key, part):
    salted = jax.random.fold_in(key, 11)
    noise_key, jitter_key = jax.random.split(salted, 2)
    noise = jnp.clip(jax.random.normal(noise_key, (TOKENS, D), jnp.float32), -4.0, 4.0)
    jitter = jax.random.uniform(jitter_key, (D,), jnp.float32)
    exponent = jnp.arange(D, dtype=jnp.float32) / D - 0.5 + 0.2 * (jitter - 0.5)
    scales = 10.0 ** exponent
    return (scales[None, :] * noise).astype(jnp.bfloat16)


def draw_hidden_acts(key, part):
    salted = jax.random.fold_in(key, 23)
    noise_key, scale_key = jax.random.split(salted)
    noise = jnp.clip(jax.random.normal(noise_key, (TOKENS, F), jnp.float32), -4.0, 4.0)
    scales = 10.0 ** (jax.random.uniform(scale_key, (F,), jnp.float32) - 0.5)
    return (scales[None, :] * noise).astype(jnp.bfloat16)


def expert_order(key):
    return jax.random.permutation(jax.random.fold_in(key, 5), jnp.arange(EXPERTS, dtype=jnp.int32))


def draw_routing(key, part):
    order = expert_order(key)
    hot_count = N_EP - EXPERTS
    hot_rows = jnp.repeat(order[:hot_count], CAP)
    cold_pool = jnp.repeat(order[hot_count:], CAP - 1)
    cold_take = TOK_DEV - hot_count * CAP
    salted = jax.random.fold_in(key, 61)

    def one_device(index):
        device_key = jax.random.fold_in(salted, index)
        picked = jax.random.permutation(jax.random.fold_in(device_key, 1), cold_pool)[:cold_take]
        rows = jnp.concatenate([hot_rows, picked])
        return jax.random.permutation(jax.random.fold_in(device_key, 2), rows)
    table = jax.vmap(one_device)(jnp.arange(TOKENS // TOK_DEV, dtype=jnp.int32))
    return table.reshape(TOKENS, 1).astype(jnp.int32)


def draw_current_slots(key, part):
    order = expert_order(key)
    ordinal = jnp.arange(N_EP, dtype=jnp.int32)
    extra = order[jnp.clip(ordinal - EXPERTS, 0, N_EP - EXPERTS - 1)]
    filled = jnp.where(ordinal < EXPERTS, ordinal, extra)
    return jax.random.permutation(jax.random.fold_in(key, 31), filled)


def draw_next_slots(key, part):
    order = expert_order(key)
    salted = jax.random.fold_in(key, 47)
    first, second = jax.random.split(salted)
    ordinal = jnp.arange(N_EP, dtype=jnp.int32)
    picks = jax.random.randint(first, (N_EP,), 0, N_EP - EXPERTS, dtype=jnp.int32)
    extra = order[picks]
    filled = jnp.where(ordinal < EXPERTS, ordinal, extra)
    return jax.random.permutation(second, filled)


def touch_ends(result, own_key, low, largest):
    longest = result.shape.index(max(result.shape))
    spots = []
    for shift in (0, 1):
        where = [jax.random.randint(jax.random.fold_in(own_key, axis), (), 0, length) for axis, length in enumerate(result.shape)]
        where[longest] = (where[longest] + shift) % result.shape[longest]
        spots.append(tuple(where))
    return result.at[spots[0]].set(low).at[spots[1]].set(largest)


def block_levels(own_key, dims, pieces, low, largest):
    def one(dim, blocks):
        draws = jax.random.uniform(jax.random.fold_in(jax.random.fold_in(own_key, 6), dim), (blocks,), jnp.float32, low / len(pieces), largest / len(pieces))
        return jnp.repeat(jnp.exp(draws), dims[dim] // blocks).reshape((-1,) + (1,) * (len(dims) - dim - 1))

    gain = one(*pieces[0])
    for cut in pieces[1:]:
        gain = gain * one(*cut)
    return gain


def bell_draw(rng, dims, deviation, bound, shards=(), kind=jnp.bfloat16):
    level = block_levels(rng, dims, shards, -0.22, 0.18) if shards else 1.0
    drawn = jax.random.normal(rng, dims, jnp.float32) * deviation * level
    return jnp.minimum(jnp.maximum(drawn, -bound), bound).astype(kind)


def setup_inputs(seed: int = 0) -> dict:
    key_list = jax.random.split(jax.random.key(seed), 8)
    out_grads = draw_out_grads(jax.random.fold_in(key_list[7], 71), 0)
    hidden_acts = draw_hidden_acts(jax.random.fold_in(key_list[7], 71), 0)
    routing = draw_routing(jax.random.fold_in(key_list[7], 71), 0)
    replica_pick = touch_ends(jax.random.randint(key_list[3], (TOKENS,), 0, 4), jax.random.fold_in(key_list[3], 1), 0, 3).astype(jnp.int32)
    master_weights = bell_draw(key_list[4], (N_EP, D, F), F ** -0.5, 0.25, ((0, 8), (1, 4)), jnp.float32)
    current_slots = draw_current_slots(jax.random.fold_in(key_list[7], 71), 0)
    next_slots = draw_next_slots(jax.random.fold_in(key_list[7], 71), 0)
    return {"out_grads": out_grads, "hidden_acts": hidden_acts, "routing": routing, "replica_pick": replica_pick, "master_weights": master_weights, "current_slots": current_slots, "next_slots": next_slots}


POLY_FIRST = 3.4445
POLY_SECOND = -4.775
POLY_THIRD = 2.0315
LEARNING_RATE = 0.02
UPDATE_SCALE = 0.2
EPSILON = 1e-07
PRECISE = lax.Precision.HIGHEST

def slot_ranks(placement):
    number = placement.shape[0]
    matching = placement[:, None] == placement[None, :]
    earlier = jnp.arange(number, dtype=jnp.int32)[None, :] < jnp.arange(number, dtype=jnp.int32)[:, None]
    return lax.optimization_barrier(jnp.sum(matching & earlier, axis=1)).astype(jnp.int32)

def choose_slots(placement, rankings, experts_named, wanted_index):
    holders = placement[None, :] == experts_named[:, None]
    totals = lax.optimization_barrier(jnp.sum(holders, axis=1)).astype(jnp.int32)
    wanted = jnp.remainder(wanted_index, totals)
    chosen = holders & (rankings[None, :] == wanted[:, None])
    ordinal = jnp.arange(placement.shape[0], dtype=jnp.int32)[None, :]
    return lax.optimization_barrier(jnp.sum(jnp.where(chosen, ordinal, 0), axis=1)).astype(jnp.int32)

def orthogonalize(grad):
    normed = grad / (jnp.sqrt(jnp.sum(grad * grad)) + EPSILON)
    for iteration in range(NS_STEPS):
        gram_now = jnp.dot(normed.T, normed, precision=PRECISE)
        polynomial = POLY_SECOND * gram_now + POLY_THIRD * jnp.dot(gram_now, gram_now, precision=PRECISE)
        normed = POLY_FIRST * normed + jnp.dot(normed, polynomial, precision=PRECISE)
    return UPDATE_SCALE * D ** 0.5 * normed

def reference(out_grads, hidden_acts, routing, replica_pick, master_weights, current_slots, next_slots):
    rankings = slot_ranks(current_slots)
    slot_of_row = choose_slots(current_slots, rankings, routing[:, 0], replica_pick)
    devices = TOKENS // TOK_DEV
    onehot = (slot_of_row.reshape(devices, TOK_DEV)[:, :, None] == jnp.arange(N_EP, dtype=jnp.int32)[None, None, :]).astype(jnp.int32)
    position = lax.optimization_barrier(jnp.sum(onehot * (jnp.cumsum(onehot, axis=1) - 1), axis=2)).reshape(-1).astype(jnp.int32)
    row_ids = jnp.arange(TOKENS, dtype=jnp.int32)
    device_of_row = row_ids // TOK_DEV
    source_ep = device_of_row // N_DP
    group_of_row = device_of_row % N_DP
    within = (group_of_row * (N_EP * CAP) + source_ep * CAP + position).astype(jnp.int32)
    inverse = jnp.full((N_EP, N_DP * N_EP * CAP), TOKENS, jnp.int32).at[slot_of_row, within].set(row_ids)
    grads_padded = jnp.concatenate([out_grads, jnp.zeros((1, D), out_grads.dtype)], axis=0)
    acts_padded = jnp.concatenate([hidden_acts, jnp.zeros((1, F), hidden_acts.dtype)], axis=0)

    def per_slot(operands):
        index, weight = operands
        rows_grads = grads_padded[index]
        rows_acts = acts_padded[index]
        back = jnp.dot(rows_grads, weight.astype(jnp.bfloat16), preferred_element_type=jnp.float32)

        def group_partial(pair):
            part_grads, part_acts = pair
            return jnp.dot(part_grads.T, part_acts, preferred_element_type=jnp.float32)
        partials = lax.map(group_partial, (rows_grads.reshape(N_DP, -1, D), rows_acts.reshape(N_DP, -1, F)))
        return (back, lax.optimization_barrier(jnp.sum(partials, axis=0)))
    backs, slot_grads = lax.map(per_slot, (inverse, master_weights))
    input_grads = backs[slot_of_row, within]
    expert_grads = jax.ops.segment_sum(slot_grads, current_slots, num_segments=EXPERTS)
    updates = lax.map(orthogonalize, expert_grads)
    experts_all = jnp.arange(EXPERTS, dtype=jnp.int32)
    homes = choose_slots(current_slots, rankings, experts_all, jnp.zeros_like(experts_all))
    fresh = master_weights[homes] - LEARNING_RATE * updates
    return (input_grads, fresh[next_slots], updates[next_slots])
```

```python
import functools

import jax
import jax.numpy as jnp
from jax import lax
from jax.experimental import pallas as pl
from jax.experimental.pallas import tpu as pltpu
from jax.sharding import PartitionSpec as P

NS_STEPS = 2
POLY_FIRST = 3.4445
POLY_SECOND = -4.775
POLY_THIRD = 2.0315
LEARNING_RATE = 0.02
UPDATE_SCALE = 0.2
EPSILON = 1e-07
LANES = 128
GATHER_BYTES = 4 << 20
BF = jnp.bfloat16
F32 = jnp.float32
VMEM = pl.BlockSpec(memory_space=pltpu.VMEM)
SMEM = pl.BlockSpec(memory_space=pltpu.SMEM)


def call(body, outs, flops, moved, *operands):
    scalar_first = operands[0].ndim == 1
    specs = [SMEM if scalar_first and i == 0 else VMEM for i in range(len(operands))]
    return pl.pallas_call(
        body,
        out_shape=outs,
        in_specs=specs,
        out_specs=jax.tree.map(lambda _: VMEM, outs),
        cost_estimate=pl.CostEstimate(flops=flops, bytes_accessed=moved, transcendentals=0),
    )(*operands)


def dot(a, b):
    return jnp.dot(a, b, preferred_element_type=F32)


def dot_rows(a, b):
    return lax.dot_general(a, b, (((0,), (0,)), ((), ())), preferred_element_type=F32)


def halves(x):
    high = x.astype(BF)
    return high, (x - high.astype(F32)).astype(BF)


def dot3(a, b, product=dot):
    return product(a[0], b[0]) + (product(a[0], b[1]) + product(a[1], b[0]))


def iota(shape, axis):
    return lax.broadcasted_iota(jnp.int32, shape, axis)


def column(row):
    size = row.shape[1]
    eye = iota((size, size), 0) == iota((size, size), 1)
    return jnp.sum(jnp.where(eye, row, 0), axis=1, keepdims=True)


def pack_body(capacity, meta, routing, pick, current, following, grads, acts, payload, across, mine, theirs):
    rows, width = grads.shape
    slots = current.shape[1]
    parts = payload.shape[0]
    block = width // parts
    hidden = acts.shape[1]
    half = payload.shape[2] - block
    named = routing[...]
    held = current[...]
    held_column = column(held)
    before = iota((slots, slots), 1) < iota((slots, slots), 0)
    rank = jnp.sum(jnp.where((held_column == held) & before, 1, 0), axis=1, keepdims=True)
    holds = held_column == named
    total = jnp.sum(jnp.where(holds, 1, 0), axis=0, keepdims=True)
    wanted = jnp.where(total > 1, pick[...] & 1, 0)
    slot = jnp.sum(
        jnp.where(holds & (rank == wanted), iota((slots, rows), 0), 0), axis=0, keepdims=True
    )
    earlier = iota((rows, rows), 0) < iota((rows, rows), 1)
    position = jnp.sum(
        jnp.where((column(named) == named) & earlier, 1, 0), axis=0, keepdims=True
    )
    places = slots * capacity
    place = iota((places, slots), 0) // capacity == iota((places, slots), 1)
    wants = jnp.sum(jnp.where(place, following[...], 0), axis=1, keepdims=True)
    inside = lax.rem(iota((places, 1), 0), capacity)
    chosen = jnp.where((wants == named) & (inside == position), 1.0, 0.0).astype(BF)
    picked_acts = dot(chosen, acts[...]).astype(BF)
    for part in range(parts):
        payload[part, :, :block] = dot(chosen, grads[:, part * block : (part + 1) * block]).astype(BF)
        low = part % (hidden // half) * half
        payload[part, :, block:] = picked_acts[:, low : low + half]
    tags = jnp.broadcast_to(column(slot).astype(F32), (rows, LANES)).astype(BF)
    across[:, 2 * block :] = tags
    mine[:, block:] = tags
    theirs[:, block:] = tags
    for part in range(parts):

        @pl.when(meta[0] == part)
        def _():
            other = part ^ 1
            far = part ^ 2
            mine[:, :block] = grads[:, part * block : (part + 1) * block]
            theirs[:, :block] = grads[:, other * block : (other + 1) * block]
            across[:, :block] = grads[:, far * block : (far + 1) * block]
            far = far ^ 1
            across[:, block : 2 * block] = grads[:, far * block : (far + 1) * block]


def grad_body(meta, received, acts_other, grad, slab_own, slab_other):
    block = grad.shape[0]
    hidden = grad.shape[1]
    half = hidden // 2
    quarter = half // 2
    core = meta[0] & 1
    rows = received[:, :block]
    own = dot_rows(rows, received[:, block:])
    other = dot_rows(rows, acts_other[...])
    first = jnp.where(core == 0, own, other)
    second = jnp.where(core == 0, other, own)
    grad[:, :half] = first
    grad[:, half:] = second
    first, second = halves(first), halves(second)
    top = dot3(first, first, dot_rows)
    cross = dot3(first, second, dot_rows)
    low = dot3(second, second, dot_rows)
    slab_own[:, :half] = jnp.where(core == 0, top, low)
    slab_other[:, :half] = jnp.where(core == 0, low, top)
    slab_own[:, half:] = jnp.where(core == 0, cross[:, :quarter], cross[:, quarter:])
    slab_other[:, half:] = jnp.where(core == 0, cross[:, quarter:], cross[:, :quarter])


def newton_body(scale, meta, slab_own, slab_other, grad, update, gram):
    hidden = grad.shape[1]
    half = hidden // 2
    quarter = half // 2
    core = meta[0] & 1
    own, other = slab_own[...], slab_other[...]
    first = jnp.where(core == 0, own, other)
    second = jnp.where(core == 0, other, own)
    gram[:half, :half] = first[:, :half]
    gram[half:, half:] = second[:, :half]
    gram[:half, half : half + quarter] = first[:, half:]
    gram[:half, half + quarter :] = second[:, half:]
    gram[half : half + quarter, :half] = first[:, half:].T
    gram[half + quarter :, :half] = second[:, half:].T
    eye = iota((hidden, hidden), 0) == iota((hidden, hidden), 1)
    total = gram[...]
    squares = jnp.sum(jnp.sum(jnp.where(eye, total, 0.0), axis=1, keepdims=True), axis=0, keepdims=True)
    inverse = 1.0 / (jnp.sqrt(squares) + EPSILON)
    now = (total * inverse) * inverse
    chain = None
    for step in range(NS_STEPS):
        split = halves(now)
        factor = POLY_SECOND * now + POLY_THIRD * dot3(split, split)
        factor = factor + jnp.where(eye, POLY_FIRST, 0.0)
        parts = halves(factor)
        chain = parts if chain is None else halves(dot3(chain, parts))
        if step + 1 < NS_STEPS:
            now = dot3(halves(dot3(split, parts)), parts)
    normed = halves(grad[...] * inverse)
    update[...] = scale * dot3(normed, chain)


def route_body(near, meta, rows, rows_far, *refs):
    weights, (keep, send) = refs[:near], refs[near:]
    block = weights[0].shape[0]
    half = rows.shape[0] // 2
    for index, source in enumerate((rows, rows_far)):
        data = source[:, :block]
        tag = source[:, block:][:, :1].astype(F32)
        total = None
        for k in range(near):
            mask = tag == meta[4 + k].astype(F32)
            term = dot(jnp.where(mask, data, jnp.zeros_like(data)), weights[k][...])
            total = term if total is None else total + term
        keep[index * half : (index + 1) * half, :] = total[:half]
        send[index * half : (index + 1) * half, :] = total[half:]


def select_body(near, meta, *refs):
    weights, chosen = refs[:near], refs[near]
    for k in range(near):

        @pl.when(meta[3] == k)
        def _():
            chosen[...] = weights[k][...]


def finish_body(near, meta, *refs):
    weights, (arrived, update, fresh) = refs[:near], refs[near:]
    step = LEARNING_RATE * update[...]
    for k in range(near + 1):

        @pl.when(meta[2] == k)
        def _():
            source = weights[k] if k < near else arrived
            fresh[...] = source[...].astype(F32) - step


def partner(size, bit):
    return [(i, i ^ bit) for i in range(size)]


def exchange(x, axis, bit):
    return lax.ppermute(x, axis, partner(lax.axis_size(axis), bit))


def describe(current, following, near):
    slots = current.shape[0]
    me = lax.axis_index("ep")
    entry = jnp.arange(4 + near, dtype=jnp.int32)
    ask = jnp.where(entry == 3, me ^ 1, me)
    index = jnp.arange(slots, dtype=jnp.int32)
    hit = (current[None, None, :] == following[None, :, None]) & (
        index[None, :, None] == ask[:, None, None]
    )
    home = jnp.min(jnp.where(hit, index[None, None, :], slots), axis=(1, 2))
    steps = lax.rem(me // 2 - home // 2 + near, near)
    local = (home & 1) == (me & 1)
    ring = lax.rem(me // 2 - (entry - 4) + near, near) * 2 + (me & 1)
    values = jnp.where(entry == 2, jnp.where(local, steps, near), steps)
    values = jnp.where(entry == 0, lax.axis_index("dp"), values)
    values = jnp.where(entry == 1, me, values)
    return jnp.where(entry >= 4, ring, values).astype(jnp.int32)


def per_device(
    out_grads, hidden_acts, routing, replica_pick, master_weights, current_slots, next_slots
):
    rows, width = out_grads.shape
    hidden = hidden_acts.shape[1]
    slots, parts = lax.axis_size("ep"), lax.axis_size("dp")
    capacity = 2 * rows // slots
    block = width // parts
    half = hidden // 2
    near = slots // 2
    master = master_weights[0]
    gather = near * block * hidden * 2 <= GATHER_BYTES
    meta = describe(current_slots, next_slots, near if gather else 1)
    shape = jax.ShapeDtypeStruct
    payload, across, mine, theirs = call(
        functools.partial(pack_body, capacity),
        (
            shape((parts, slots * capacity, block + half), BF),
            shape((rows, 2 * block + LANES), BF),
            shape((rows, block + LANES), BF),
            shape((rows, block + LANES), BF),
        ),
        4 * rows * rows * (width + hidden),
        8 * rows * width,
        meta,
        routing.reshape(1, rows),
        replica_pick.reshape(1, rows),
        current_slots.reshape(1, slots),
        next_slots.reshape(1, slots),
        out_grads,
        hidden_acts,
    )
    received = lax.all_to_all(
        payload.reshape(parts * slots, capacity, block + half),
        ("dp", "ep"),
        split_axis=0,
        concat_axis=0,
        tiled=True,
    ).reshape(parts * slots * capacity, block + half)
    if gather:
        input_grads, finish = gathered(meta, across, mine, theirs, master, near)
    else:
        input_grads, finish = routed(
            out_grads, routing, replica_pick, master, current_slots, next_slots, hidden
        )

    acts_other = exchange(received[:, block:], "dp", 1)
    tall = received.shape[0]
    grad, slab_own, slab_other = call(
        grad_body,
        (
            shape((block, hidden), F32),
            shape((half, half + half // 2), F32),
            shape((half, half + half // 2), F32),
        ),
        2 * tall * block * hidden + 6 * block * hidden * hidden,
        4 * block * hidden,
        meta,
        received,
        acts_other,
    )
    slab = slab_own + exchange(slab_other, "dp", 1)
    slab = slab + exchange(slab, "dp", 2)
    slab_other = exchange(slab, "dp", 1)
    update = pl.pallas_call(
        functools.partial(newton_body, UPDATE_SCALE * width**0.5),
        out_shape=shape((block, hidden), F32),
        in_specs=[SMEM, VMEM, VMEM, VMEM],
        out_specs=VMEM,
        scratch_shapes=[pltpu.VMEM((hidden, hidden), F32)],
        cost_estimate=pl.CostEstimate(
            flops=36 * hidden**3, bytes_accessed=8 * hidden * hidden, transcendentals=0
        ),
    )(meta, slab, slab_other, grad)
    return (input_grads, finish(update)[None], update[None])


def gathered(meta, across, mine, theirs, master, near):
    rows = mine.shape[0]
    block, hidden = master.shape
    slots, parts = lax.axis_size("ep"), lax.axis_size("dp")
    shape = jax.ShapeDtypeStruct
    turn = [(i, (i + 2) % slots) for i in range(slots)]
    weights = [master.astype(BF)]
    for _ in range(near - 1):
        weights.append(lax.ppermute(weights[-1], "ep", turn))
    beside = exchange(across, "dp", 2)
    passed = exchange(jnp.concatenate([theirs, beside[:, block:]], axis=0), "dp", 1)
    kept = jnp.concatenate(
        [
            mine,
            jnp.concatenate([beside[:, :block], beside[:, 2 * block :]], axis=1),
            passed,
        ],
        axis=0,
    )
    far = exchange(kept, "ep", 1)
    total = 4 * rows
    keep, send = call(
        functools.partial(route_body, near),
        (shape((total, hidden), F32), shape((total, hidden), F32)),
        4 * total * near * block * hidden,
        4 * total * hidden * 4,
        meta,
        kept,
        far,
        *weights,
    )
    summed = (keep + exchange(send, "dp", 1)).reshape(4, rows, hidden)
    small = summed.astype(BF)
    diagonal = [
        (e * parts + d, (e ^ 1) * parts + (d ^ 2)) for e in range(slots) for d in range(parts)
    ]
    by_x = exchange(small[1], "dp", 2)
    by_y = exchange(small[2], "ep", 1)
    by_both = lax.ppermute(small[3], ("ep", "dp"), diagonal)
    input_grads = summed[0] + by_x.astype(F32) + (by_y.astype(F32) + by_both.astype(F32))

    wanted = call(
        functools.partial(select_body, near),
        shape((block, hidden), BF),
        0,
        4 * block * hidden,
        meta,
        *weights,
    )
    arrived = exchange(wanted, "ep", 1)

    def finish(update):
        return call(
            functools.partial(finish_body, near),
            shape((block, hidden), F32),
            2 * block * hidden,
            10 * block * hidden,
            meta,
            *weights,
            arrived,
            update,
        )

    return input_grads, finish


def routed(out_grads, routing, replica_pick, master, current, following, hidden):
    rows, width = out_grads.shape
    slots = lax.axis_size("ep")
    capacity = 2 * rows // slots
    number = jnp.arange(slots, dtype=jnp.int32)
    swap = functools.partial(
        lax.all_to_all, axis_name="ep", split_axis=0, concat_axis=0, tiled=True
    )
    rank = jnp.sum((current[:, None] == current[None, :]) & (number[None, :] < number[:, None]), axis=1)
    holds = current[None, :] == routing
    wanted = jnp.remainder(replica_pick, jnp.sum(holds, axis=1))
    slot = jnp.sum(jnp.where(holds & (rank[None, :] == wanted[:, None]), number[None, :], 0), axis=1)
    onehot = (slot[:, None] == number[None, :]).astype(jnp.int32)
    position = jnp.sum(onehot * (jnp.cumsum(onehot, axis=0) - 1), axis=1)
    target = slot * capacity + position
    sent = jnp.zeros((slots * capacity, width), BF).at[target].set(out_grads)
    taken = swap(sent.reshape(slots, capacity, width)).reshape(-1, width)
    whole = lax.all_gather(master.astype(BF), "dp", axis=0, tiled=True)
    product = dot(taken, whole).reshape(slots, capacity, hidden)
    input_grads = swap(product).reshape(-1, hidden)[target]
    spread = swap(master.reshape(slots, -1))
    match = current[None, :] == following[:, None]
    home = jnp.min(jnp.where(match, number[None, :], slots), axis=1)
    arrived = swap(jnp.take(spread, home, axis=0)).reshape(master.shape)
    return input_grads, lambda update: arrived - LEARNING_RATE * update


def solution(mesh):
    placed = (
        P(("ep", "dp"), None),
        P(("ep", "dp"), None),
        P(("ep", "dp"), None),
        P(("ep", "dp")),
        P("ep", "dp", None),
        P(),
        P(),
    )
    return jax.shard_map(
        per_device,
        mesh=mesh,
        in_specs=placed,
        out_specs=(P(("ep", "dp"), None), P("ep", "dp", None), P("ep", "dp", None)),
        check_vma=False,
    )
```

```python
import functools

import jax
import jax.numpy as jnp
from jax import lax
from jax.experimental import pallas as pl
from jax.experimental.pallas import tpu as pltpu
from jax.sharding import PartitionSpec as P


NS_STEPS = 2
POLY_FIRST = 3.4445
POLY_SECOND = -4.775
POLY_THIRD = 2.0315
LEARNING_RATE = 0.02
UPDATE_SCALE = 0.2
EPSILON = 1e-07
LANES = 128
LINE = 4
ARRIVALS = 6
BF = jnp.bfloat16
F32 = jnp.float32
VMEM = pl.BlockSpec(memory_space=pltpu.VMEM)
SMEM = pl.BlockSpec(memory_space=pltpu.SMEM)
GRANT = pltpu.CompilerParams(vmem_limit_bytes=16 << 20)


def call(body, outs, flops, moved, *operands):
    scalar_first = operands[0].ndim == 1
    specs = [SMEM if scalar_first and i == 0 else VMEM for i in range(len(operands))]
    return pl.pallas_call(
        body,
        out_shape=outs,
        in_specs=specs,
        out_specs=jax.tree.map(lambda _: VMEM, outs),
        compiler_params=GRANT,
        cost_estimate=pl.CostEstimate(flops=flops, bytes_accessed=moved, transcendentals=0),
    )(*operands)


def dot(a, b):
    return jnp.dot(a, b, preferred_element_type=F32)


def dot_rows(a, b):
    return lax.dot_general(a, b, (((0,), (0,)), ((), ())), preferred_element_type=F32)


def halves(x):
    high = x.astype(BF)
    return high, (x - high.astype(F32)).astype(BF)


def dot3(a, b):
    left = jnp.concatenate((a[0], a[0], a[1]), axis=1)
    return dot(left, jnp.concatenate((b[0], b[1], b[0]), axis=0))


def dot3_rows(a, b):
    left = jnp.concatenate((a[0], a[0], a[1]), axis=0)
    return dot_rows(left, jnp.concatenate((b[0], b[1], b[0]), axis=0))


def iota(shape, axis):
    return lax.broadcasted_iota(jnp.int32, shape, axis)


def column(row):
    size = row.shape[1]
    eye = iota((size, size), 0) == iota((size, size), 1)
    return jnp.sum(jnp.where(eye, row, 0), axis=1, keepdims=True)


def pack_body(capacity, place_dp, *refs):
    far, (payload, across, mine, theirs), near = refs[:6], refs[6:10], refs[10:16]
    sems = refs[16]
    for index, (source, target) in enumerate(zip(far, near)):
        pltpu.make_async_copy(source, target, sems.at[index]).start()
    for index, (source, target) in enumerate(zip(far, near)):
        pltpu.make_async_copy(source, target, sems.at[index]).wait()
    routing, pick, current, following, grads, acts = near
    rows, width = grads.shape
    slots = current.shape[1]
    parts = payload.shape[0]
    block = width // parts
    hidden = acts.shape[1]
    quarter = hidden // parts
    named = routing[...]
    held = current[...]
    held_column = column(held)
    before = iota((slots, slots), 1) < iota((slots, slots), 0)
    rank = jnp.sum(jnp.where((held_column == held) & before, 1, 0), axis=1, keepdims=True)
    holds = held_column == named
    total = jnp.sum(jnp.where(holds, 1, 0), axis=0, keepdims=True)
    wanted = jnp.where(total > 1, pick[...] & 1, 0)
    slot = jnp.sum(
        jnp.where(holds & (rank == wanted), iota((slots, rows), 0), 0), axis=0, keepdims=True
    )
    earlier = iota((rows, rows), 0) < iota((rows, rows), 1)
    position = jnp.sum(
        jnp.where((column(named) == named) & earlier, 1, 0), axis=0, keepdims=True
    )
    places = slots * capacity
    place = iota((places, slots), 0) // capacity == iota((places, slots), 1)
    wants = jnp.sum(jnp.where(place, following[...], 0), axis=1, keepdims=True)
    inside = lax.rem(iota((places, 1), 0), capacity)
    chosen = jnp.where((wants == named) & (inside == position), 1.0, 0.0).astype(BF)
    picked_acts = dot(chosen, acts[...]).astype(BF)
    for part in range(parts):
        payload[part, :, :block] = dot(chosen, grads[:, part * block : (part + 1) * block]).astype(BF)
        payload[part, :, block:] = picked_acts[:, part * quarter : (part + 1) * quarter]
    tags = jnp.broadcast_to(column(slot).astype(F32), (rows, LANES)).astype(BF)
    across[:, 2 * block :] = tags
    mine[:, block:] = tags
    theirs[:, block:] = tags
    for part in range(parts):

        @pl.when(place_dp[0] == part)
        def _():
            other = part ^ 1
            far = part ^ 2
            mine[:, :block] = grads[:, part * block : (part + 1) * block]
            theirs[:, :block] = grads[:, other * block : (other + 1) * block]
            across[:, :block] = grads[:, far * block : (far + 1) * block]
            far = far ^ 1
            across[:, block : 2 * block] = grads[:, far * block : (far + 1) * block]


def grad_body(meta, received, acts_pair, acts_core, grad, slab_own, slab_other):
    block, hidden = grad.shape
    half = hidden // 2
    quarter = half // 2
    place = meta[0]
    core = place & 1
    rows = received[:, :block]
    for source, flip in ((acts_pair, 0), (acts_core, 1)):
        mixed = dot_rows(rows, source[...])
        for index in (0, 1):
            where = pl.multiple_of((place ^ flip ^ (2 * index)) * quarter, quarter)
            grad[:, pl.ds(where, quarter)] = mixed[:, index * quarter : (index + 1) * quarter]
    first, second = halves(grad[:, :half]), halves(grad[:, half:])
    top = dot3_rows(first, first)
    cross = dot3_rows(first, second)
    low = dot3_rows(second, second)
    slab_own[:, :half] = jnp.where(core == 0, top, low)
    slab_other[:, :half] = jnp.where(core == 0, low, top)
    slab_own[:, half:] = jnp.where(core == 0, cross[:, :quarter], cross[:, quarter:])
    slab_other[:, half:] = jnp.where(core == 0, cross[:, quarter:], cross[:, :quarter])


def newton_body(scale, meta, slab_own, slab_other, grad, update, change, gram):
    hidden = grad.shape[1]
    half = hidden // 2
    quarter = half // 2
    core = meta[0] & 1
    own, other = slab_own[...], slab_other[...]
    first = jnp.where(core == 0, own, other)
    second = jnp.where(core == 0, other, own)
    gram[:half, :half] = first[:, :half]
    gram[half:, half:] = second[:, :half]
    gram[:half, half : half + quarter] = first[:, half:]
    gram[:half, half + quarter :] = second[:, half:]
    gram[half : half + quarter, :half] = first[:, half:].T
    gram[half + quarter :, :half] = second[:, half:].T
    eye = iota((hidden, hidden), 0) == iota((hidden, hidden), 1)
    total = gram[...]
    squares = jnp.sum(jnp.sum(jnp.where(eye, total, 0.0), axis=1, keepdims=True), axis=0, keepdims=True)
    inverse = 1.0 / (jnp.sqrt(squares) + EPSILON)
    now = (total * inverse) * inverse
    chain = None
    for step in range(NS_STEPS):
        split = halves(now)
        factor = POLY_SECOND * now + POLY_THIRD * dot3(split, split)
        factor = factor + jnp.where(eye, POLY_FIRST, 0.0)
        parts = halves(factor)
        chain = parts if chain is None else halves(dot3(chain, parts))
        if step + 1 < NS_STEPS:
            now = dot3(halves(dot3(split, parts)), parts)
    normed = halves(grad[...] * inverse)
    moved = scale * dot3(normed, chain)
    update[...] = moved
    change[...] = LEARNING_RATE * moved


def route_body(first, groups, meta, rows, rows_far, *refs):
    weights, (keep, send) = refs[:-2], refs[-2:]
    half = rows.shape[0] // 2
    block = weights[0].shape[0]

    def product(group):
        for index, source in enumerate((rows, rows_far)):
            tag = source[:, block : block + 1].astype(F32)
            data = source[:, :block]
            term = None
            for k in group:
                mask = tag == meta[4 + k].astype(F32)
                part = dot(jnp.where(mask, data, jnp.zeros_like(data)), weights[k - first][...])
                term = part if term is None else term + part
            low, high = index * half, (index + 1) * half
            keep[low:high, :] = term[:half]
            send[low:high, :] = term[half:]

    for chosen, (test, group) in enumerate(groups):
        here = meta[4 + test] >= 0

        @pl.when(here if chosen == 0 else jnp.logical_not(meta[4 + groups[0][0]] >= 0))
        def _():
            product(group)


def select_body(indices, count, meta, *refs):
    weights, chosen = refs[:count], refs[count:]
    for index, target in zip(indices, chosen):
        for k in range(count):

            @pl.when(meta[index] == k)
            def _():
                target[...] = weights[k][...]

        @pl.when(meta[index] == count)
        def _():
            target[...] = jnp.zeros_like(target)


def partner(size, bit):
    return [(i, i ^ bit) for i in range(size)]


def exchange(x, axis, bit):
    return lax.ppermute(x, axis, partner(lax.axis_size(axis), bit))


def describe(current, following):
    slots = current.shape[0]
    me = lax.axis_index("ep")
    line = me // 2
    inside = (line == 1) | (line == 2)
    entry = jnp.arange(4 + ARRIVALS, dtype=jnp.int32)
    ask = jnp.where(entry == 3, me ^ 1, me)
    index = jnp.arange(slots, dtype=jnp.int32)
    hit = (current[None, None, :] == following[None, :, None]) & (
        index[None, :, None] == ask[:, None, None]
    )
    home = jnp.min(jnp.where(hit, index[None, None, :], slots), axis=(1, 2))
    apart = line ^ (home // 2)
    held = jnp.where(inside, jnp.where(apart == 2, 3, 2), jnp.where(apart == 2, 4, 5))
    held = jnp.where(apart < 2, apart, held)
    here = (home & 1) == (me & 1)
    values = jnp.where(here, held, ARRIVALS)
    values = jnp.where(entry == 0, lax.axis_index("dp"), values)
    arrival = entry - 4
    flip = jnp.where(arrival < 2, arrival, jnp.where((arrival == 2) | (arrival == 5), 3, 2))
    comes = (arrival < 2) | (inside == (arrival < 4))
    source = jnp.where(comes, me ^ (2 * flip), -1)
    return jnp.where(entry >= 4, source, values).astype(jnp.int32)


def whole_step(
    out_grads, hidden_acts, routing, replica_pick, master_weights, current_slots, next_slots
):
    rows, width = out_grads.shape
    hidden = hidden_acts.shape[1]
    slots, parts = lax.axis_size("ep"), lax.axis_size("dp")
    capacity = 2 * rows // slots
    places = slots * capacity
    block, quarter, half = width // parts, hidden // parts, hidden // 2
    near = slots // 2
    master = master_weights[0]
    gather = near == LINE
    shape = jax.ShapeDtypeStruct
    operands = (
        routing.reshape(1, rows),
        replica_pick.reshape(1, rows),
        current_slots.reshape(1, slots),
        next_slots.reshape(1, slots),
        out_grads,
        hidden_acts,
    )
    payload, across, mine, theirs = pl.pallas_call(
        functools.partial(pack_body, capacity),
        out_shape=(
            shape((parts, places, block + quarter), BF),
            shape((rows, 2 * block + LANES), BF),
            shape((rows, block + LANES), BF),
            shape((rows, block + LANES), BF),
        ),
        in_specs=[SMEM] + [pl.BlockSpec(memory_space=pltpu.HBM)] * len(operands),
        out_specs=(VMEM,) * 4,
        scratch_shapes=[pltpu.VMEM(x.shape, x.dtype) for x in operands]
        + [pltpu.SemaphoreType.DMA((len(operands),))],
        compiler_params=GRANT,
        cost_estimate=pl.CostEstimate(
            flops=4 * rows * rows * (width + hidden),
            bytes_accessed=8 * rows * width,
            transcendentals=0,
        ),
    )(jnp.full((1,), lax.axis_index("dp"), jnp.int32), *operands)
    received = lax.all_to_all(
        payload.reshape(parts * slots, capacity, block + quarter),
        ("dp", "ep"),
        split_axis=0,
        concat_axis=0,
        tiled=True,
    ).reshape(parts * places, block + quarter)
    meta = describe(current_slots, next_slots)
    if gather:
        input_grads, finish = gathered(meta, across, mine, theirs, master)
    else:
        input_grads, finish = routed(
            out_grads, routing, replica_pick, master, current_slots, next_slots, hidden
        )

    acts = received[:, block:]
    acts = jnp.concatenate([acts, exchange(acts, "dp", 2)], axis=1)
    acts_core = exchange(acts, "dp", 1)
    tall = received.shape[0]
    grad, slab_own, slab_other = call(
        grad_body,
        (
            shape((block, hidden), F32),
            shape((half, half + half // 2), F32),
            shape((half, half + half // 2), F32),
        ),
        2 * tall * block * hidden + 6 * block * hidden * hidden,
        4 * block * hidden,
        meta,
        received,
        acts,
        acts_core,
    )
    slab = slab_own + exchange(slab_other, "dp", 1)
    slab = slab + exchange(slab.astype(BF), "dp", 2).astype(F32)
    slab_other = exchange(slab, "dp", 1)
    update, change = pl.pallas_call(
        functools.partial(newton_body, UPDATE_SCALE * width**0.5),
        out_shape=(shape((block, hidden), F32), shape((block, hidden), F32)),
        in_specs=[SMEM, VMEM, VMEM, VMEM],
        out_specs=(VMEM, VMEM),
        scratch_shapes=[pltpu.VMEM((hidden, hidden), F32)],
        compiler_params=GRANT,
        cost_estimate=pl.CostEstimate(
            flops=36 * hidden**3, bytes_accessed=8 * hidden * hidden, transcendentals=0
        ),
    )(meta, slab, slab_other, grad)
    return (input_grads, finish(change)[None], update[None])


def gathered(meta, across, mine, theirs, master):
    rows = mine.shape[0]
    block, hidden = master.shape
    slots, parts = lax.axis_size("ep"), lax.axis_size("dp")
    shape = jax.ShapeDtypeStruct

    def send(x, steps):
        pairs = [(2 * a + i, 2 * b + i) for a, b in steps for i in (0, 1)]
        return lax.ppermute(x, "ep", pairs)

    own = master.astype(BF)
    beside_line = send(own, [(0, 1), (1, 0), (2, 3), (3, 2)])
    inner = send(own, [(1, 2), (2, 1)])
    inner_far = send(beside_line, [(1, 2), (2, 1)])
    outer = send(inner, [(1, 0), (2, 3)])
    outer_far = send(own, [(0, 3), (3, 0)])
    weights = [own, beside_line, inner, inner_far, outer, outer_far]
    beside = exchange(across, "dp", 2)
    passed = exchange(jnp.concatenate([theirs, beside[:, block:]], axis=0), "dp", 1)
    kept = jnp.concatenate(
        [
            mine,
            jnp.concatenate([beside[:, :block], beside[:, 2 * block :]], axis=1),
            passed,
        ],
        axis=0,
    )
    far = exchange(kept, "ep", 1)
    total = 4 * rows
    both = (shape((total, hidden), F32), shape((total, hidden), F32))
    work = 4 * total * block * hidden

    def route(first, last, groups):
        return call(
            functools.partial(route_body, first, groups),
            both,
            work * (last - first),
            4 * total * hidden * 4,
            meta,
            kept,
            far,
            *weights[first:last],
        )

    keep, send_on = route(0, 3, ((2, (0, 1, 2)), (0, (0, 1))))
    early = keep + exchange(send_on, "dp", 1)
    keep, send_on = route(3, ARRIVALS, ((3, (3,)), (4, (4, 5))))
    summed = early + (keep + exchange(send_on, "dp", 1))
    summed = summed.reshape(4, rows, hidden)
    small = summed.astype(BF)
    diagonal = [
        (e * parts + d, (e ^ 1) * parts + (d ^ 2)) for e in range(slots) for d in range(parts)
    ]
    by_x = exchange(small[1], "dp", 2)
    by_y = exchange(small[2], "ep", 1)
    by_both = lax.ppermute(small[3], ("ep", "dp"), diagonal)
    input_grads = summed[0] + by_x.astype(F32) + (by_y.astype(F32) + by_both.astype(F32))

    wanted, ours = call(
        functools.partial(select_body, (3, 2), ARRIVALS),
        (shape((block, hidden), BF), shape((block, hidden), BF)),
        0,
        8 * block * hidden,
        meta,
        *weights,
    )
    arrived = exchange(wanted, "ep", 1)

    def finish(change):
        return (ours.astype(F32) + arrived.astype(F32)) - change

    return input_grads, finish


def routed(out_grads, routing, replica_pick, master, current, following, hidden):
    rows, width = out_grads.shape
    slots = lax.axis_size("ep")
    capacity = 2 * rows // slots
    number = jnp.arange(slots, dtype=jnp.int32)
    swap = functools.partial(
        lax.all_to_all, axis_name="ep", split_axis=0, concat_axis=0, tiled=True
    )
    rank = jnp.sum((current[:, None] == current[None, :]) & (number[None, :] < number[:, None]), axis=1)
    holds = current[None, :] == routing
    wanted = jnp.remainder(replica_pick, jnp.sum(holds, axis=1))
    slot = jnp.sum(jnp.where(holds & (rank[None, :] == wanted[:, None]), number[None, :], 0), axis=1)
    onehot = (slot[:, None] == number[None, :]).astype(jnp.int32)
    position = jnp.sum(onehot * (jnp.cumsum(onehot, axis=0) - 1), axis=1)
    target = slot * capacity + position
    sent = jnp.zeros((slots * capacity, width), BF).at[target].set(out_grads)
    taken = swap(sent.reshape(slots, capacity, width)).reshape(-1, width)
    whole = lax.all_gather(master.astype(BF), "dp", axis=0, tiled=True)
    product = dot(taken, whole).reshape(slots, capacity, hidden)
    input_grads = swap(product).reshape(-1, hidden)[target]
    spread = swap(master.reshape(slots, -1))
    match = current[None, :] == following[:, None]
    home = jnp.min(jnp.where(match, number[None, :], slots), axis=1)
    arrived = swap(jnp.take(spread, home, axis=0)).reshape(master.shape)
    return input_grads, lambda change: arrived - change


def solution(mesh):
    placed = (
        P(("ep", "dp"), None),
        P(("ep", "dp"), None),
        P(("ep", "dp"), None),
        P(("ep", "dp")),
        P("ep", "dp", None),
        P(),
        P(),
    )
    return jax.shard_map(
        whole_step,
        mesh=mesh,
        in_specs=placed,
        out_specs=(P(("ep", "dp"), None), P("ep", "dp", None), P("ep", "dp", None)),
        check_vma=False,
    )
```

```python
import functools

import jax
import jax.numpy as jnp
from jax import lax
from jax.experimental import pallas as pl
from jax.experimental.pallas import tpu as pltpu
from jax.sharding import PartitionSpec as P


NS_STEPS = 2
POLY_FIRST = 3.4445
POLY_SECOND = -4.775
POLY_THIRD = 2.0315
LEARNING_RATE = 0.02
UPDATE_SCALE = 0.2
EPSILON = 1e-07
LANES = 128
LINE = 4
ARRIVALS = 6
BF = jnp.bfloat16
F32 = jnp.float32
VMEM = pl.BlockSpec(memory_space=pltpu.VMEM)
SMEM = pl.BlockSpec(memory_space=pltpu.SMEM)
GRANT = pltpu.CompilerParams(vmem_limit_bytes=16 << 20)


def call(body, outs, flops, moved, *operands):
    scalar_first = operands[0].ndim == 1
    specs = [SMEM if scalar_first and i == 0 else VMEM for i in range(len(operands))]
    return pl.pallas_call(
        body,
        out_shape=outs,
        in_specs=specs,
        out_specs=jax.tree.map(lambda _: VMEM, outs),
        compiler_params=GRANT,
        cost_estimate=pl.CostEstimate(flops=flops, bytes_accessed=moved, transcendentals=0),
    )(*operands)


def dot(a, b):
    return jnp.dot(a, b, preferred_element_type=F32)


def dot_rows(a, b):
    return lax.dot_general(a, b, (((0,), (0,)), ((), ())), preferred_element_type=F32)


def halves(x):
    high = x.astype(BF)
    return high, (x - high.astype(F32)).astype(BF)


def dot3(a, b):
    left = jnp.concatenate((a[0], a[0], a[1]), axis=1)
    return dot(left, jnp.concatenate((b[0], b[1], b[0]), axis=0))


def dot3_rows(a, b):
    left = jnp.concatenate((a[0], a[0], a[1]), axis=0)
    return dot_rows(left, jnp.concatenate((b[0], b[1], b[0]), axis=0))


def iota(shape, axis):
    return lax.broadcasted_iota(jnp.int32, shape, axis)


def column(row):
    size = row.shape[1]
    eye = iota((size, size), 0) == iota((size, size), 1)
    return jnp.sum(jnp.where(eye, row, 0), axis=1, keepdims=True)


def pack_body(capacity, place_dp, *refs):
    far, (payload, across, mine, theirs), near = refs[:6], refs[6:10], refs[10:16]
    sems = refs[16]
    for index, (source, target) in enumerate(zip(far, near)):
        pltpu.make_async_copy(source, target, sems.at[index]).start()

    def wait(low, high):
        for index in range(low, high):
            pltpu.make_async_copy(far[index], near[index], sems.at[index]).wait()

    wait(0, 4)
    routing, pick, current, following, grads, acts = near
    rows, width = grads.shape
    slots = current.shape[1]
    parts = payload.shape[0]
    block = width // parts
    hidden = acts.shape[1]
    quarter = hidden // parts
    named = routing[...]
    held = current[...]
    held_column = column(held)
    before = iota((slots, slots), 1) < iota((slots, slots), 0)
    rank = jnp.sum(jnp.where((held_column == held) & before, 1, 0), axis=1, keepdims=True)
    holds = held_column == named
    total = jnp.sum(jnp.where(holds, 1, 0), axis=0, keepdims=True)
    wanted = jnp.where(total > 1, pick[...] & 1, 0)
    slot = jnp.sum(
        jnp.where(holds & (rank == wanted), iota((slots, rows), 0), 0), axis=0, keepdims=True
    )
    earlier = iota((rows, rows), 0) < iota((rows, rows), 1)
    position = jnp.sum(
        jnp.where((column(named) == named) & earlier, 1, 0), axis=0, keepdims=True
    )
    places = slots * capacity
    place = iota((places, slots), 0) // capacity == iota((places, slots), 1)
    wants = jnp.sum(jnp.where(place, following[...], 0), axis=1, keepdims=True)
    inside = lax.rem(iota((places, 1), 0), capacity)
    chosen = jnp.where((wants == named) & (inside == position), 1.0, 0.0).astype(BF)
    wait(4, 6)
    picked_acts = dot(chosen, acts[...]).astype(BF)
    for part in range(parts):
        payload[part, :, :block] = dot(chosen, grads[:, part * block : (part + 1) * block]).astype(BF)
        payload[part, :, block:] = picked_acts[:, part * quarter : (part + 1) * quarter]
    tags = jnp.broadcast_to(column(slot).astype(F32), (rows, LANES)).astype(BF)
    across[:, 2 * block :] = tags
    mine[:, block:] = tags
    theirs[:, block:] = tags
    for part in range(parts):

        @pl.when(place_dp[0] == part)
        def _():
            other = part ^ 1
            far = part ^ 2
            mine[:, :block] = grads[:, part * block : (part + 1) * block]
            theirs[:, :block] = grads[:, other * block : (other + 1) * block]
            across[:, :block] = grads[:, far * block : (far + 1) * block]
            far = far ^ 1
            across[:, block : 2 * block] = grads[:, far * block : (far + 1) * block]


def grad_body(meta, received, acts_pair, acts_core, grad, slab_own, slab_other):
    block, hidden = grad.shape
    half = hidden // 2
    quarter = half // 2
    place = meta[0]
    core = place & 1
    rows = received[:, :block]
    for source, flip in ((acts_pair, 0), (acts_core, 1)):
        mixed = dot_rows(rows, source[...])
        for index in (0, 1):
            where = pl.multiple_of((place ^ flip ^ (2 * index)) * quarter, quarter)
            grad[:, pl.ds(where, quarter)] = mixed[:, index * quarter : (index + 1) * quarter]
    first, second = halves(grad[:, :half]), halves(grad[:, half:])
    top = dot3_rows(first, first)
    cross = dot3_rows(first, second)
    low = dot3_rows(second, second)
    slab_own[:, :half] = jnp.where(core == 0, top, low)
    slab_other[:, :half] = jnp.where(core == 0, low, top)
    slab_own[:, half:] = jnp.where(core == 0, cross[:, :quarter], cross[:, quarter:])
    slab_other[:, half:] = jnp.where(core == 0, cross[:, quarter:], cross[:, :quarter])


def newton_body(scale, meta, slab_own, slab_other, grad, update, change, gram):
    hidden = grad.shape[1]
    half = hidden // 2
    quarter = half // 2
    core = meta[0] & 1
    own, other = slab_own[...], slab_other[...]
    first = jnp.where(core == 0, own, other)
    second = jnp.where(core == 0, other, own)
    gram[:half, :half] = first[:, :half]
    gram[half:, half:] = second[:, :half]
    gram[:half, half : half + quarter] = first[:, half:]
    gram[:half, half + quarter :] = second[:, half:]
    gram[half : half + quarter, :half] = first[:, half:].T
    gram[half + quarter :, :half] = second[:, half:].T
    eye = iota((hidden, hidden), 0) == iota((hidden, hidden), 1)
    total = gram[...]
    squares = jnp.sum(jnp.sum(jnp.where(eye, total, 0.0), axis=1, keepdims=True), axis=0, keepdims=True)
    inverse = 1.0 / (jnp.sqrt(squares) + EPSILON)
    now = (total * inverse) * inverse
    chain = None
    for step in range(NS_STEPS):
        split = halves(now)
        factor = POLY_SECOND * now + POLY_THIRD * dot3(split, split)
        factor = factor + jnp.where(eye, POLY_FIRST, 0.0)
        parts = halves(factor)
        chain = parts if chain is None else halves(dot3(chain, parts))
        if step + 1 < NS_STEPS:
            now = dot3(halves(dot3(split, parts)), parts)
    normed = halves(grad[...] * inverse)
    moved = scale * dot3(normed, chain)
    update[...] = moved
    change[...] = LEARNING_RATE * moved


def route_body(first, groups, meta, rows, rows_far, *refs):
    weights, (keep, send) = refs[:-2], refs[-2:]
    half = rows.shape[0] // 2
    block = weights[0].shape[0]

    def product(group):
        for index, source in enumerate((rows, rows_far)):
            tag = source[:, block : block + 1].astype(F32)
            data = source[:, :block]
            term = None
            for k in group:
                mask = tag == meta[4 + k].astype(F32)
                part = dot(jnp.where(mask, data, jnp.zeros_like(data)), weights[k - first][...])
                term = part if term is None else term + part
            low, high = index * half, (index + 1) * half
            keep[low:high, :] = term[:half]
            send[low:high, :] = term[half:]

    for chosen, (test, group) in enumerate(groups):
        here = meta[4 + test] >= 0

        @pl.when(here if chosen == 0 else jnp.logical_not(meta[4 + groups[0][0]] >= 0))
        def _():
            product(group)


def select_body(indices, count, meta, *refs):
    weights, chosen = refs[:count], refs[count:]
    for index, target in zip(indices, chosen):
        for k in range(count):

            @pl.when(meta[index] == k)
            def _():
                target[...] = weights[k][...]

        @pl.when(meta[index] == count)
        def _():
            target[...] = jnp.zeros_like(target)


def partner(size, bit):
    return [(i, i ^ bit) for i in range(size)]


def exchange(x, axis, bit):
    return lax.ppermute(x, axis, partner(lax.axis_size(axis), bit))


def describe(current, following):
    slots = current.shape[0]
    me = lax.axis_index("ep")
    line = me // 2
    inside = (line == 1) | (line == 2)
    entry = jnp.arange(4 + ARRIVALS, dtype=jnp.int32)
    ask = jnp.where(entry == 3, me ^ 1, me)
    index = jnp.arange(slots, dtype=jnp.int32)
    hit = (current[None, None, :] == following[None, :, None]) & (
        index[None, :, None] == ask[:, None, None]
    )
    home = jnp.min(jnp.where(hit, index[None, None, :], slots), axis=(1, 2))
    apart = line ^ (home // 2)
    held = jnp.where(inside, jnp.where(apart == 2, 3, 2), jnp.where(apart == 2, 4, 5))
    held = jnp.where(apart < 2, apart, held)
    here = (home & 1) == (me & 1)
    values = jnp.where(here, held, ARRIVALS)
    values = jnp.where(entry == 0, lax.axis_index("dp"), values)
    arrival = entry - 4
    flip = jnp.where(arrival < 2, arrival, jnp.where((arrival == 2) | (arrival == 5), 3, 2))
    comes = (arrival < 2) | (inside == (arrival < 4))
    source = jnp.where(comes, me ^ (2 * flip), -1)
    return jnp.where(entry >= 4, source, values).astype(jnp.int32)


def whole_step(
    out_grads, hidden_acts, routing, replica_pick, master_weights, current_slots, next_slots
):
    rows, width = out_grads.shape
    hidden = hidden_acts.shape[1]
    slots, parts = lax.axis_size("ep"), lax.axis_size("dp")
    capacity = 2 * rows // slots
    places = slots * capacity
    block, quarter, half = width // parts, hidden // parts, hidden // 2
    near = slots // 2
    master = master_weights[0]
    gather = near == LINE
    shape = jax.ShapeDtypeStruct
    operands = (
        routing.reshape(1, rows),
        replica_pick.reshape(1, rows),
        current_slots.reshape(1, slots),
        next_slots.reshape(1, slots),
        out_grads,
        hidden_acts,
    )
    payload, across, mine, theirs = pl.pallas_call(
        functools.partial(pack_body, capacity),
        out_shape=(
            shape((parts, places, block + quarter), BF),
            shape((rows, 2 * block + LANES), BF),
            shape((rows, block + LANES), BF),
            shape((rows, block + LANES), BF),
        ),
        in_specs=[SMEM] + [pl.BlockSpec(memory_space=pltpu.HBM)] * len(operands),
        out_specs=(VMEM,) * 4,
        scratch_shapes=[pltpu.VMEM(x.shape, x.dtype) for x in operands]
        + [pltpu.SemaphoreType.DMA((len(operands),))],
        compiler_params=GRANT,
        cost_estimate=pl.CostEstimate(
            flops=4 * rows * rows * (width + hidden),
            bytes_accessed=8 * rows * width,
            transcendentals=0,
        ),
    )(jnp.full((1,), lax.axis_index("dp"), jnp.int32), *operands)
    received = lax.all_to_all(
        payload.reshape(parts * slots, capacity, block + quarter),
        ("dp", "ep"),
        split_axis=0,
        concat_axis=0,
        tiled=True,
    ).reshape(parts * places, block + quarter)
    meta = describe(current_slots, next_slots)
    if gather:
        input_grads, finish = gathered(meta, across, mine, theirs, master)
    else:
        input_grads, finish = routed(
            out_grads, routing, replica_pick, master, current_slots, next_slots, hidden
        )

    acts = received[:, block:]
    acts = jnp.concatenate([acts, exchange(acts, "dp", 2)], axis=1)
    acts_core = exchange(acts, "dp", 1)
    tall = received.shape[0]
    grad, slab_own, slab_other = call(
        grad_body,
        (
            shape((block, hidden), F32),
            shape((half, half + half // 2), F32),
            shape((half, half + half // 2), F32),
        ),
        2 * tall * block * hidden + 6 * block * hidden * hidden,
        4 * block * hidden,
        meta,
        received,
        acts,
        acts_core,
    )
    slab = slab_own + exchange(slab_other, "dp", 1)
    slab = slab + exchange(slab.astype(BF), "dp", 2).astype(F32)
    slab_other = exchange(slab, "dp", 1)
    update, change = pl.pallas_call(
        functools.partial(newton_body, UPDATE_SCALE * width**0.5),
        out_shape=(shape((block, hidden), F32), shape((block, hidden), F32)),
        in_specs=[SMEM, VMEM, VMEM, VMEM],
        out_specs=(VMEM, VMEM),
        scratch_shapes=[pltpu.VMEM((hidden, hidden), F32)],
        compiler_params=GRANT,
        cost_estimate=pl.CostEstimate(
            flops=36 * hidden**3, bytes_accessed=8 * hidden * hidden, transcendentals=0
        ),
    )(meta, slab, slab_other, grad)
    return (input_grads, finish(change)[None], update[None])


def gathered(meta, across, mine, theirs, master):
    rows = mine.shape[0]
    block, hidden = master.shape
    slots, parts = lax.axis_size("ep"), lax.axis_size("dp")
    shape = jax.ShapeDtypeStruct

    def send(x, steps):
        pairs = [(2 * a + i, 2 * b + i) for a, b in steps for i in (0, 1)]
        return lax.ppermute(x, "ep", pairs)

    def cast_body(source, target):
        target[...] = source[...].astype(BF)

    own = call(cast_body, shape((block, hidden), BF), 0, 6 * block * hidden, master)
    beside_line = send(own, [(0, 1), (1, 0), (2, 3), (3, 2)])
    inner = send(own, [(1, 2), (2, 1)])
    inner_far = send(beside_line, [(1, 2), (2, 1)])
    outer = send(inner, [(1, 0), (2, 3)])
    outer_far = send(own, [(0, 3), (3, 0)])
    weights = [own, beside_line, inner, inner_far, outer, outer_far]
    beside = exchange(across, "dp", 2)
    passed = exchange(jnp.concatenate([theirs, beside[:, block:]], axis=0), "dp", 1)
    kept = jnp.concatenate(
        [
            mine,
            jnp.concatenate([beside[:, :block], beside[:, 2 * block :]], axis=1),
            passed,
        ],
        axis=0,
    )
    far = exchange(kept, "ep", 1)
    total = 4 * rows
    both = (shape((total, hidden), F32), shape((total, hidden), F32))
    work = 4 * total * block * hidden

    def route(first, last, groups):
        return call(
            functools.partial(route_body, first, groups),
            both,
            work * (last - first),
            4 * total * hidden * 4,
            meta,
            kept,
            far,
            *weights[first:last],
        )

    keep, send_on = route(0, 3, ((2, (0, 1, 2)), (0, (0, 1))))
    early = keep + exchange(send_on, "dp", 1)
    keep, send_on = route(3, ARRIVALS, ((3, (3,)), (4, (4, 5))))
    summed = early + (keep + exchange(send_on, "dp", 1))
    summed = summed.reshape(4, rows, hidden)
    small = summed.astype(BF)
    diagonal = [
        (e * parts + d, (e ^ 1) * parts + (d ^ 2)) for e in range(slots) for d in range(parts)
    ]
    by_x = exchange(small[1], "dp", 2)
    by_y = exchange(small[2], "ep", 1)
    by_both = lax.ppermute(small[3], ("ep", "dp"), diagonal)
    input_grads = summed[0] + by_x.astype(F32) + (by_y.astype(F32) + by_both.astype(F32))

    wanted, ours = call(
        functools.partial(select_body, (3, 2), ARRIVALS),
        (shape((block, hidden), BF), shape((block, hidden), BF)),
        0,
        8 * block * hidden,
        meta,
        *weights,
    )
    arrived = exchange(wanted, "ep", 1)

    def finish(change):
        return (ours.astype(F32) + arrived.astype(F32)) - change

    return input_grads, finish


def routed(out_grads, routing, replica_pick, master, current, following, hidden):
    rows, width = out_grads.shape
    slots = lax.axis_size("ep")
    capacity = 2 * rows // slots
    number = jnp.arange(slots, dtype=jnp.int32)
    swap = functools.partial(
        lax.all_to_all, axis_name="ep", split_axis=0, concat_axis=0, tiled=True
    )
    rank = jnp.sum((current[:, None] == current[None, :]) & (number[None, :] < number[:, None]), axis=1)
    holds = current[None, :] == routing
    wanted = jnp.remainder(replica_pick, jnp.sum(holds, axis=1))
    slot = jnp.sum(jnp.where(holds & (rank[None, :] == wanted[:, None]), number[None, :], 0), axis=1)
    onehot = (slot[:, None] == number[None, :]).astype(jnp.int32)
    position = jnp.sum(onehot * (jnp.cumsum(onehot, axis=0) - 1), axis=1)
    target = slot * capacity + position
    sent = jnp.zeros((slots * capacity, width), BF).at[target].set(out_grads)
    taken = swap(sent.reshape(slots, capacity, width)).reshape(-1, width)
    whole = lax.all_gather(master.astype(BF), "dp", axis=0, tiled=True)
    product = dot(taken, whole).reshape(slots, capacity, hidden)
    input_grads = swap(product).reshape(-1, hidden)[target]
    spread = swap(master.reshape(slots, -1))
    match = current[None, :] == following[:, None]
    home = jnp.min(jnp.where(match, number[None, :], slots), axis=1)
    arrived = swap(jnp.take(spread, home, axis=0)).reshape(master.shape)
    return input_grads, lambda change: arrived - change


def solution(mesh):
    placed = (
        P(("ep", "dp"), None),
        P(("ep", "dp"), None),
        P(("ep", "dp"), None),
        P(("ep", "dp")),
        P("ep", "dp", None),
        P(),
        P(),
    )
    return jax.shard_map(
        whole_step,
        mesh=mesh,
        in_specs=placed,
        out_specs=(P(("ep", "dp"), None), P("ep", "dp", None), P("ep", "dp", None)),
        check_vma=False,
    )
```

```python
import functools

import jax
import jax.numpy as jnp
from jax import lax
from jax.experimental import pallas as pl
from jax.experimental.pallas import tpu as pltpu
from jax.sharding import PartitionSpec as P


NS_STEPS = 2
POLY_FIRST = 3.4445
POLY_SECOND = -4.775
POLY_THIRD = 2.0315
LEARNING_RATE = 0.02
UPDATE_SCALE = 0.2
EPSILON = 1e-07
LANES = 128
LINE = 4
ARRIVALS = 6
BF = jnp.bfloat16
F32 = jnp.float32
VMEM = pl.BlockSpec(memory_space=pltpu.VMEM)
SMEM = pl.BlockSpec(memory_space=pltpu.SMEM)
GRANT = pltpu.CompilerParams(vmem_limit_bytes=16 << 20)


def call(body, outs, flops, moved, *operands):
    scalar_first = operands[0].ndim == 1
    specs = [SMEM if scalar_first and i == 0 else VMEM for i in range(len(operands))]
    return pl.pallas_call(
        body,
        out_shape=outs,
        in_specs=specs,
        out_specs=jax.tree.map(lambda _: VMEM, outs),
        compiler_params=GRANT,
        cost_estimate=pl.CostEstimate(flops=flops, bytes_accessed=moved, transcendentals=0),
    )(*operands)


def dot(a, b):
    return jnp.dot(a, b, preferred_element_type=F32)


def dot_rows(a, b):
    return lax.dot_general(a, b, (((0,), (0,)), ((), ())), preferred_element_type=F32)


def halves(x):
    high = x.astype(BF)
    return high, (x - high.astype(F32)).astype(BF)


def dot3(a, b):
    left = jnp.concatenate((a[0], a[0], a[1]), axis=1)
    return dot(left, jnp.concatenate((b[0], b[1], b[0]), axis=0))


def dot3_rows(a, b):
    left = jnp.concatenate((a[0], a[0], a[1]), axis=0)
    return dot_rows(left, jnp.concatenate((b[0], b[1], b[0]), axis=0))


def iota(shape, axis):
    return lax.broadcasted_iota(jnp.int32, shape, axis)


def column(row):
    size = row.shape[1]
    eye = iota((size, size), 0) == iota((size, size), 1)
    return jnp.sum(jnp.where(eye, row, 0), axis=1, keepdims=True)


def pack_body(capacity, place_dp, *refs):
    far, (payload, across, mine, theirs), near = refs[:6], refs[6:10], refs[10:16]
    sems = refs[16]
    for index, (source, target) in enumerate(zip(far, near)):
        pltpu.make_async_copy(source, target, sems.at[index]).start()

    def wait(low, high):
        for index in range(low, high):
            pltpu.make_async_copy(far[index], near[index], sems.at[index]).wait()

    wait(0, 4)
    routing, pick, current, following, grads, acts = near
    rows, width = grads.shape
    slots = current.shape[1]
    parts = payload.shape[0]
    block = width // parts
    hidden = acts.shape[1]
    quarter = hidden // parts
    named = routing[...]
    held = current[...]
    held_column = column(held)
    before = iota((slots, slots), 1) < iota((slots, slots), 0)
    rank = jnp.sum(jnp.where((held_column == held) & before, 1, 0), axis=1, keepdims=True)
    holds = held_column == named
    total = jnp.sum(jnp.where(holds, 1, 0), axis=0, keepdims=True)
    wanted = jnp.where(total > 1, pick[...] & 1, 0)
    slot = jnp.sum(
        jnp.where(holds & (rank == wanted), iota((slots, rows), 0), 0), axis=0, keepdims=True
    )
    earlier = iota((rows, rows), 0) < iota((rows, rows), 1)
    position = jnp.sum(
        jnp.where((column(named) == named) & earlier, 1, 0), axis=0, keepdims=True
    )
    places = slots * capacity
    place = iota((places, slots), 0) // capacity == iota((places, slots), 1)
    wants = jnp.sum(jnp.where(place, following[...], 0), axis=1, keepdims=True)
    inside = lax.rem(iota((places, 1), 0), capacity)
    chosen = jnp.where((wants == named) & (inside == position), 1.0, 0.0).astype(BF)
    wait(4, 6)
    picked_acts = dot(chosen, acts[...]).astype(BF)
    for part in range(parts):
        payload[part, :, :block] = dot(chosen, grads[:, part * block : (part + 1) * block]).astype(BF)
        payload[part, :, block:] = picked_acts[:, part * quarter : (part + 1) * quarter]
    tags = jnp.broadcast_to(column(slot).astype(F32), (rows, LANES)).astype(BF)
    across[:, 2 * block :] = tags
    mine[:, block:] = tags
    theirs[:, block:] = tags
    for part in range(parts):

        @pl.when(place_dp[0] == part)
        def _():
            other = part ^ 1
            far = part ^ 2
            mine[:, :block] = grads[:, part * block : (part + 1) * block]
            theirs[:, :block] = grads[:, other * block : (other + 1) * block]
            across[:, :block] = grads[:, far * block : (far + 1) * block]
            far = far ^ 1
            across[:, block : 2 * block] = grads[:, far * block : (far + 1) * block]


def grad_body(meta, received, acts_pair, acts_core, grad, slab_own, slab_other):
    block, hidden = grad.shape
    half = hidden // 2
    quarter = half // 2
    place = meta[0]
    core = place & 1
    rows = received[:, :block]
    for source, flip in ((acts_pair, 0), (acts_core, 1)):
        mixed = dot_rows(rows, source[...])
        for index in (0, 1):
            where = pl.multiple_of((place ^ flip ^ (2 * index)) * quarter, quarter)
            grad[:, pl.ds(where, quarter)] = mixed[:, index * quarter : (index + 1) * quarter]
    first, second = halves(grad[:, :half]), halves(grad[:, half:])
    top = dot3_rows(first, first)
    cross = dot3_rows(first, second)
    low = dot3_rows(second, second)
    slab_own[:, :half] = jnp.where(core == 0, top, low)
    slab_other[:, :half] = jnp.where(core == 0, low, top)
    slab_own[:, half:] = jnp.where(core == 0, cross[:, :quarter], cross[:, quarter:])
    slab_other[:, half:] = jnp.where(core == 0, cross[:, quarter:], cross[:, :quarter])


def newton_body(scale, meta, slab_own, slab_other, grad, update, change, gram):
    hidden = grad.shape[1]
    half = hidden // 2
    quarter = half // 2
    core = meta[0] & 1
    own, other = slab_own[...], slab_other[...]
    first = jnp.where(core == 0, own, other)
    second = jnp.where(core == 0, other, own)
    gram[:half, :half] = first[:, :half]
    gram[half:, half:] = second[:, :half]
    gram[:half, half : half + quarter] = first[:, half:]
    gram[:half, half + quarter :] = second[:, half:]
    gram[half : half + quarter, :half] = first[:, half:].T
    gram[half + quarter :, :half] = second[:, half:].T
    eye = iota((hidden, hidden), 0) == iota((hidden, hidden), 1)
    total = gram[...]
    squares = jnp.sum(jnp.sum(jnp.where(eye, total, 0.0), axis=1, keepdims=True), axis=0, keepdims=True)
    inverse = 1.0 / (jnp.sqrt(squares) + EPSILON)
    now = (total * inverse) * inverse
    chain = None
    for step in range(NS_STEPS):
        split = halves(now)
        factor = POLY_SECOND * now + POLY_THIRD * dot3(split, split)
        factor = factor + jnp.where(eye, POLY_FIRST, 0.0)
        parts = halves(factor)
        chain = parts if chain is None else halves(dot3(chain, parts))
        if step + 1 < NS_STEPS:
            now = dot3(halves(dot3(split, parts)), parts)
    normed = halves(grad[...] * inverse)
    moved = scale * dot3(normed, chain)
    update[...] = moved
    change[...] = LEARNING_RATE * moved


def route_body(first, groups, outs, meta, rows, rows_far, *refs):
    weights, targets = refs[: -len(outs)], refs[-len(outs) :]
    half = rows.shape[0] // 2
    begin, end = outs[0] * half, (outs[-1] + 1) * half
    block = weights[0].shape[0]

    def product(group):
        for index, source in enumerate((rows, rows_far)):
            tag = source[begin:end, block : block + 1].astype(F32)
            data = source[begin:end, :block]
            term = None
            for k in group:
                mask = tag == meta[4 + k].astype(F32)
                part = dot(jnp.where(mask, data, jnp.zeros_like(data)), weights[k - first][...])
                term = part if term is None else term + part
            low, high = index * half, (index + 1) * half
            for place, target in enumerate(targets):
                target[low:high, :] = term[place * half : (place + 1) * half]

    for chosen, (test, group) in enumerate(groups):
        here = meta[4 + test] >= 0

        @pl.when(here if chosen == 0 else jnp.logical_not(meta[4 + groups[0][0]] >= 0))
        def _():
            product(group)


def select_body(indices, count, meta, *refs):
    weights, chosen = refs[:count], refs[count:]
    for index, target in zip(indices, chosen):
        for k in range(count):

            @pl.when(meta[index] == k)
            def _():
                target[...] = weights[k][...]

        @pl.when(meta[index] == count)
        def _():
            target[...] = jnp.zeros_like(target)


def partner(size, bit):
    return [(i, i ^ bit) for i in range(size)]


def exchange(x, axis, bit):
    return lax.ppermute(x, axis, partner(lax.axis_size(axis), bit))


def describe(current, following):
    slots = current.shape[0]
    me = lax.axis_index("ep")
    line = me // 2
    inside = (line == 1) | (line == 2)
    entry = jnp.arange(4 + ARRIVALS, dtype=jnp.int32)
    ask = jnp.where(entry == 3, me ^ 1, me)
    index = jnp.arange(slots, dtype=jnp.int32)
    hit = (current[None, None, :] == following[None, :, None]) & (
        index[None, :, None] == ask[:, None, None]
    )
    home = jnp.min(jnp.where(hit, index[None, None, :], slots), axis=(1, 2))
    apart = line ^ (home // 2)
    held = jnp.where(inside, jnp.where(apart == 2, 3, 2), jnp.where(apart == 2, 4, 5))
    held = jnp.where(apart < 2, apart, held)
    here = (home & 1) == (me & 1)
    values = jnp.where(here, held, ARRIVALS)
    values = jnp.where(entry == 0, lax.axis_index("dp"), values)
    arrival = entry - 4
    flip = jnp.where(arrival < 2, arrival, jnp.where((arrival == 2) | (arrival == 5), 3, 2))
    comes = (arrival < 2) | (inside == (arrival < 4))
    source = jnp.where(comes, me ^ (2 * flip), -1)
    return jnp.where(entry >= 4, source, values).astype(jnp.int32)


def whole_step(
    out_grads, hidden_acts, routing, replica_pick, master_weights, current_slots, next_slots
):
    rows, width = out_grads.shape
    hidden = hidden_acts.shape[1]
    slots, parts = lax.axis_size("ep"), lax.axis_size("dp")
    capacity = 2 * rows // slots
    places = slots * capacity
    block, quarter, half = width // parts, hidden // parts, hidden // 2
    near = slots // 2
    master = master_weights[0]
    gather = near == LINE
    shape = jax.ShapeDtypeStruct
    operands = (
        routing.reshape(1, rows),
        replica_pick.reshape(1, rows),
        current_slots.reshape(1, slots),
        next_slots.reshape(1, slots),
        out_grads,
        hidden_acts,
    )
    payload, across, mine, theirs = pl.pallas_call(
        functools.partial(pack_body, capacity),
        out_shape=(
            shape((parts, places, block + quarter), BF),
            shape((rows, 2 * block + LANES), BF),
            shape((rows, block + LANES), BF),
            shape((rows, block + LANES), BF),
        ),
        in_specs=[SMEM] + [pl.BlockSpec(memory_space=pltpu.HBM)] * len(operands),
        out_specs=(VMEM,) * 4,
        scratch_shapes=[pltpu.VMEM(x.shape, x.dtype) for x in operands]
        + [pltpu.SemaphoreType.DMA((len(operands),))],
        compiler_params=GRANT,
        cost_estimate=pl.CostEstimate(
            flops=4 * rows * rows * (width + hidden),
            bytes_accessed=8 * rows * width,
            transcendentals=0,
        ),
    )(jnp.full((1,), lax.axis_index("dp"), jnp.int32), *operands)
    received = lax.all_to_all(
        payload.reshape(parts * slots, capacity, block + quarter),
        ("dp", "ep"),
        split_axis=0,
        concat_axis=0,
        tiled=True,
    ).reshape(parts * places, block + quarter)
    meta = describe(current_slots, next_slots)
    if gather:
        input_grads, finish = gathered(meta, across, mine, theirs, master)
    else:
        input_grads, finish = routed(
            out_grads, routing, replica_pick, master, current_slots, next_slots, hidden
        )

    acts = received[:, block:]
    acts = jnp.concatenate([acts, exchange(acts, "dp", 2)], axis=1)
    acts_core = exchange(acts, "dp", 1)
    tall = received.shape[0]
    grad, slab_own, slab_other = call(
        grad_body,
        (
            shape((block, hidden), F32),
            shape((half, half + half // 2), F32),
            shape((half, half + half // 2), F32),
        ),
        2 * tall * block * hidden + 6 * block * hidden * hidden,
        4 * block * hidden,
        meta,
        received,
        acts,
        acts_core,
    )
    slab = slab_own + exchange(slab_other, "dp", 1)
    slab = slab + exchange(slab.astype(BF), "dp", 2).astype(F32)
    slab_other = exchange(slab, "dp", 1)
    update, change = pl.pallas_call(
        functools.partial(newton_body, UPDATE_SCALE * width**0.5),
        out_shape=(shape((block, hidden), F32), shape((block, hidden), F32)),
        in_specs=[SMEM, VMEM, VMEM, VMEM],
        out_specs=(VMEM, VMEM),
        scratch_shapes=[pltpu.VMEM((hidden, hidden), F32)],
        compiler_params=GRANT,
        cost_estimate=pl.CostEstimate(
            flops=36 * hidden**3, bytes_accessed=8 * hidden * hidden, transcendentals=0
        ),
    )(meta, slab, slab_other, grad)
    return (input_grads, finish(change)[None], update[None])


def gathered(meta, across, mine, theirs, master):
    rows = mine.shape[0]
    block, hidden = master.shape
    slots, parts = lax.axis_size("ep"), lax.axis_size("dp")
    shape = jax.ShapeDtypeStruct

    def send(x, steps):
        pairs = [(2 * a + i, 2 * b + i) for a, b in steps for i in (0, 1)]
        return lax.ppermute(x, "ep", pairs)

    def cast_body(source, target):
        target[...] = source[...].astype(BF)

    own = call(cast_body, shape((block, hidden), BF), 0, 6 * block * hidden, master)
    beside_line = send(own, [(0, 1), (1, 0), (2, 3), (3, 2)])
    inner = send(own, [(1, 2), (2, 1)])
    inner_far = send(beside_line, [(1, 2), (2, 1)])
    outer = send(inner, [(1, 0), (2, 3)])
    outer_far = send(own, [(0, 3), (3, 0)])
    weights = [own, beside_line, inner, inner_far, outer, outer_far]
    beside = exchange(across, "dp", 2)
    passed = exchange(jnp.concatenate([theirs, beside[:, block:]], axis=0), "dp", 1)
    kept = jnp.concatenate(
        [
            mine,
            jnp.concatenate([beside[:, :block], beside[:, 2 * block :]], axis=1),
            passed,
        ],
        axis=0,
    )
    far = exchange(kept, "ep", 1)
    total = 4 * rows
    work = 4 * total * block * hidden

    def route(first, last, groups, outs=(0, 1)):
        return call(
            functools.partial(route_body, first, groups, outs),
            tuple(shape((total, hidden), F32) for _ in outs),
            work * (last - first) * len(outs) // 2,
            2 * len(outs) * total * hidden * 4,
            meta,
            kept,
            far,
            *weights[first:last],
        )

    keep, send_on = route(0, 3, ((2, (0, 1, 2)), (0, (0, 1))))
    early = keep + exchange(send_on, "dp", 1)
    late = ((3, (3,)), (4, (4, 5)))
    (send_on,) = route(3, ARRIVALS, late, (1,))
    (keep,) = route(3, ARRIVALS, late, (0,))
    summed = early + (keep + exchange(send_on, "dp", 1))
    summed = summed.reshape(4, rows, hidden)
    small = summed.astype(BF)
    diagonal = [
        (e * parts + d, (e ^ 1) * parts + (d ^ 2)) for e in range(slots) for d in range(parts)
    ]
    by_x = exchange(small[1], "dp", 2)
    by_y = exchange(small[2], "ep", 1)
    by_both = lax.ppermute(small[3], ("ep", "dp"), diagonal)
    input_grads = summed[0] + by_x.astype(F32) + (by_y.astype(F32) + by_both.astype(F32))

    def select(index):
        (chosen,) = call(
            functools.partial(select_body, (index,), ARRIVALS),
            (shape((block, hidden), BF),),
            0,
            4 * block * hidden,
            meta,
            *weights,
        )
        return chosen

    wanted, ours = select(3), select(2)
    arrived = exchange(wanted, "ep", 1)

    def finish(change):
        return (ours.astype(F32) + arrived.astype(F32)) - change

    return input_grads, finish


def routed(out_grads, routing, replica_pick, master, current, following, hidden):
    rows, width = out_grads.shape
    slots = lax.axis_size("ep")
    capacity = 2 * rows // slots
    number = jnp.arange(slots, dtype=jnp.int32)
    swap = functools.partial(
        lax.all_to_all, axis_name="ep", split_axis=0, concat_axis=0, tiled=True
    )
    rank = jnp.sum((current[:, None] == current[None, :]) & (number[None, :] < number[:, None]), axis=1)
    holds = current[None, :] == routing
    wanted = jnp.remainder(replica_pick, jnp.sum(holds, axis=1))
    slot = jnp.sum(jnp.where(holds & (rank[None, :] == wanted[:, None]), number[None, :], 0), axis=1)
    onehot = (slot[:, None] == number[None, :]).astype(jnp.int32)
    position = jnp.sum(onehot * (jnp.cumsum(onehot, axis=0) - 1), axis=1)
    target = slot * capacity + position
    sent = jnp.zeros((slots * capacity, width), BF).at[target].set(out_grads)
    taken = swap(sent.reshape(slots, capacity, width)).reshape(-1, width)
    whole = lax.all_gather(master.astype(BF), "dp", axis=0, tiled=True)
    product = dot(taken, whole).reshape(slots, capacity, hidden)
    input_grads = swap(product).reshape(-1, hidden)[target]
    spread = swap(master.reshape(slots, -1))
    match = current[None, :] == following[:, None]
    home = jnp.min(jnp.where(match, number[None, :], slots), axis=1)
    arrived = swap(jnp.take(spread, home, axis=0)).reshape(master.shape)
    return input_grads, lambda change: arrived - change


def solution(mesh):
    placed = (
        P(("ep", "dp"), None),
        P(("ep", "dp"), None),
        P(("ep", "dp"), None),
        P(("ep", "dp")),
        P("ep", "dp", None),
        P(),
        P(),
    )
    return jax.shard_map(
        whole_step,
        mesh=mesh,
        in_specs=placed,
        out_specs=(P(("ep", "dp"), None), P("ep", "dp", None), P("ep", "dp", None)),
        check_vma=False,
    )
```
